256 devices in a mesh: section: 16 (over z, core), inner: 16 (over y, x).
Axes of the slice: x: 4, y: 4, z: 8, core: 2. Of those that a mesh axis runs over, the one named last changes fastest.
Arguments:
- plant: float32 [256, 256], replicated, may hold values from 0 to 1
- actuation: float32 [256, 256], replicated, may hold values from -0.21875 to 0.21875
- state_weight: float32 [16, 256], P('section'), may hold values from 0.01 to 1
- input_weight: float32 [16, 256], P('section'), may hold values from 0.1 to 2
- state_grad: float32 [16, 256], P('section'), may hold values from -3 to 3
- input_grad: float32 [16, 256], P('section'), may hold values from -3 to 3
- defect: float32 [16, 256], P('section'), may hold values from -1.2 to 1.2
- terminal_hess: float32 [256, 256], replicated, as said below
- terminal_grad: float32 [256], replicated, may hold values from -6 to 6
Outputs:
- value_hess: float32 [16, 256, 256], P('section', 'inner')
- value_grad: float32 [16, 256], P('section', 'inner')
The draws below stay inside these ranges and needn't reach their ends.
Inputs may be any that keep to these rules, and one draw needn't show every extreme that they name: `terminal_hess`: symmetric positive definite.
All inputs are finite; a program needn't handle non-finite values.
Results may differ from the reference program's by a relative error of at most 0.0002.
Values sent between devices are 32-bit elements; how exact they have to be, the bound alone decides.
No kernel may reach another device: no remote copies, remote signals or barrier semaphores. Data moves between devices by JAX's collectives and lax.ppermute only.
A program may use at most 128 MiB of HBM per device.

```python
import math
import jax
import jax.numpy as jnp
from jax import lax

NX = 256
NU = 256
SECTIONS = 16


heat_step = 4.0


def draw_plant(key, part):
    key_face = jax.random.fold_in(key, 0)
    conduct = jnp.exp(jax.random.uniform(key_face, (NX + 1,), jnp.float32, -0.7, 0.7))
    diagonal = conduct[:-1] + conduct[1:]
    coupling = conduct[1:-1]
    laplace = jnp.diag(diagonal) - jnp.diag(coupling, 1) - jnp.diag(coupling, -1)
    system = jnp.eye(NX, dtype=jnp.float32) + heat_step * laplace
    return jnp.linalg.solve(system, jnp.eye(NX, dtype=jnp.float32))


def draw_terminal_hess(key, part):
    key_mix, key_diag = jax.random.split(key)
    mixing = jax.random.normal(key_mix, (NX, NX), jnp.float32)
    gram_part = jnp.dot(mixing, mixing.T, precision=jax.lax.Precision.HIGHEST) * (0.25 / NX)
    diagonal = jnp.exp(jax.random.uniform(key_diag, (NX,), jnp.float32, -0.7, 0.7))
    return 0.5 * (gram_part + gram_part.T) + jnp.diag(diagonal)


def block_levels(own_key, dims, cuts, smallest, largest):
    factor_of = 1.0
    for axis_at, blocks in cuts:
        draws = jax.random.uniform(jax.random.fold_in(jax.random.fold_in(own_key, 6), axis_at), (blocks,), jnp.float32, smallest / len(cuts), largest / len(cuts))
        factor_of = factor_of * jnp.repeat(jnp.exp(draws), dims[axis_at] // blocks).reshape((-1,) + (1,) * (len(dims) - 1 - axis_at))
    return factor_of


def bell_draw(stream_key, dims, scale, reach, cuts=(), held_as=jnp.bfloat16):
    gain = block_levels(stream_key, dims, cuts, -0.22, 0.18) if cuts else 1.0
    drawn = jax.random.normal(stream_key, dims, jnp.float32) * scale * gain
    return jnp.minimum(jnp.maximum(drawn, -reach), reach).astype(held_as)


def setup_inputs(seed: int = 0) -> dict:
    seeds = jax.random.split(jax.random.key(seed), 10)
    return {
        "plant": draw_plant(jax.random.fold_in(seeds[9], 71), 0),
        "actuation": bell_draw(seeds[1], (NX, NU), (3 * NX) ** -0.5, 0.21875, (), jnp.float32),
        "state_weight": jnp.clip(jnp.exp(math.log(1.0) - 4.6051702 * jax.random.uniform(seeds[2], (SECTIONS, NX), jnp.float32) ** block_levels(seeds[2], (SECTIONS, NX), ((0, 16),), -0.2, 0.2)), 0.01, 1.0),
        "input_weight": jnp.clip(jnp.exp(math.log(2.0) - 2.9957323 * jax.random.uniform(seeds[3], (SECTIONS, NU), jnp.float32) ** block_levels(seeds[3], (SECTIONS, NU), ((0, 16),), -0.2, 0.2)), 0.1, 2.0),
        "state_grad": bell_draw(seeds[4], (SECTIONS, NX), 0.5, 3.0, ((0, 16),), jnp.float32),
        "input_grad": bell_draw(seeds[5], (SECTIONS, NU), 0.5, 3.0, ((0, 16),), jnp.float32),
        "defect": bell_draw(seeds[6], (SECTIONS, NX), 0.2, 1.2, ((0, 16),), jnp.float32),
        "terminal_hess": draw_terminal_hess(jax.random.fold_in(seeds[9], 71), 0),
        "terminal_grad": bell_draw(seeds[8], (NX,), 1.0, 6.0, (), jnp.float32),
    }


highest = lax.Precision.HIGHEST

def matmul(first_mat, second_mat):
    return jnp.dot(first_mat, second_mat, precision=highest)

def reference(plant, actuation, state_weight, input_weight, state_grad, input_grad, defect, terminal_hess, terminal_grad):
    identity = jnp.eye(NX, dtype=terminal_hess.dtype)

    def backward(carried, phase_data):
        hess_next, linear_next = carried
        weights, inputs, gradient, input_gradient, defects = phase_data
        scaled = actuation / inputs[None, :]
        spread = matmul(scaled, actuation.T)
        drift_term = defects - matmul(scaled, input_gradient)
        system = identity + matmul(hess_next, spread)
        gained = jnp.linalg.solve(system, hess_next)
        hessian = matmul(matmul(plant.T, gained), plant) + jnp.diag(weights)
        carried_linear = jnp.linalg.solve(system, linear_next - matmul(hess_next, drift_term))
        linear = matmul(plant.T, carried_linear) - gradient
        return ((hessian, linear), (hessian, -linear))
    start_value = (terminal_hess, -terminal_grad)
    final_state, outputs = lax.scan(backward, start_value, (state_weight, input_weight, state_grad, input_grad, defect), reverse=True)
    return (outputs[0], outputs[1])
```

```python
import jax
import jax.numpy as jnp
from jax import lax
from jax.experimental import pallas as pl
from jax.experimental.pallas import tpu as pltpu
from jax.sharding import PartitionSpec as P

f32, bf16 = jnp.float32, jnp.bfloat16
N = 256
PHASES = 16
highest = lax.Precision.HIGHEST


def split(x):
    head = x.astype(bf16)
    return head, (x - head.astype(f32)).astype(bf16)


def dot(a, b):
    return jnp.dot(a, b, preferred_element_type=f32)


def dot3(a, b):
    (ah, al), (bh, bl) = a, b
    return dot(ah, bh) + (dot(ah, bl) + dot(al, bh))


def exact(a, b):
    return jnp.dot(a, b, precision=highest, preferred_element_type=f32)


def square_sum(x):
    return jnp.sum(jnp.sum(x * x, axis=0, keepdims=True), axis=1, keepdims=True)


def kernel(
    g_ref, plant_ref, act_ref, term_ref, tgrad_ref, hess_ref, grad_ref,
    ph_ref, plo_ref, pt_ref, pth_ref, ath_ref, atl_ref, apa_ref, eye_ref, drift_ref,
    kh_ref, kl_ref, th_ref, tl_ref, bh_ref, bl_ref, s_ref, lin_ref, bad_ref, e_ref, x_ref,
):
    section = lax.axis_index("section")
    inner = lax.axis_index("inner")
    plant = plant_ref[...]
    act = act_ref[...]
    ph_ref[...], plo_ref[...] = split(plant)
    plant_t = plant.T
    pt_ref[...] = plant_t
    pth_ref[...] = plant_t.astype(bf16)
    act_t = act.T
    ath_ref[...], atl_ref[...] = split(act_t)
    apa_ref[pl.ds(0, N), :] = act
    apa_ref[pl.ds(N, N), :] = exact(plant, act)
    rows = lax.broadcasted_iota(jnp.int32, (N, N), 0)
    cols = lax.broadcasted_iota(jnp.int32, (N, N), 1)
    eye_ref[...] = jnp.where(rows == cols, 1.0, 0.0).astype(f32)
    drift_ref[...] = g_ref[:, 4, :] - exact(g_ref[:, 3, :] / g_ref[:, 1, :], act_t)

    def start():
        eye = eye_ref[...]
        scaled = apa_ref[pl.ds(0, N), :] / g_ref[PHASES - 1][1:2]
        s = dot3(split(scaled), (ath_ref[...], atl_ref[...]))
        kh_ref[...], kl_ref[...] = split(dot3(split(term_ref[...]), split(s)))
        lin_ref[...] = -jnp.sum(eye * tgrad_ref[...], axis=1, keepdims=True)
        bad_ref[...] = jnp.zeros((1, 1), f32)

    def quick(levels):
        eye, pt = eye_ref[...], pt_ref[...]
        kh, kl = kh_ref[...], kl_ref[...]
        k = kh.astype(f32) + kl.astype(f32)
        first = dot(jnp.concatenate([kh, pth_ref[...]], axis=0), kh)
        mu = jnp.sqrt(square_sum(k)) * 0.25
        al = 2.0 / (2.0 + mu)
        rho = mu * al * 0.5
        c = 2.0 / (2.0 - rho * rho)
        x = eye * (c * al * (2.0 - al)) - (c * al * al) * k
        t = (c * al * (2.0 - al)) * pt - (c * al * al) * first[N:]
        e = eye * (1.0 - c + c * (1.0 - al) * (1.0 - al)) - (2.0 * c * al * (1.0 - al)) * k
        e = e + (c * al * al) * first[:N]
        for _ in range(1, levels):
            rho = rho * rho / (2.0 - rho * rho)
            c = 2.0 / (2.0 - rho * rho)
            eh = e.astype(bf16)
            product = dot(jnp.concatenate([eh, x.astype(bf16), t.astype(bf16)], axis=0), eh)
            e = (1.0 - c) * eye + c * product[:N]
            x = c * (x + product[N : 2 * N])
            t = c * (t + product[2 * N :])
        guess = t.astype(bf16)
        t = guess.astype(f32)
        residue = pt - t - (dot(guess, kh) + dot(guess, kl))
        good = (square_sum(e) < 2.5e-3) & (square_sum(residue) < 4e-4 * square_sum(t))
        bad_ref[...] += jnp.where(good, 0.0, 1.0)
        return t + dot(residue.astype(bf16), x.astype(bf16))

    def careful():
        eye, pt = eye_ref[...], pt_ref[...]
        k = kh_ref[...].astype(f32) + kl_ref[...].astype(f32)
        mu = jnp.minimum(jnp.sqrt(jnp.sum(k * k)), jnp.max(jnp.sum(jnp.abs(k), axis=1)))
        al = 2.0 / (2.0 + mu)
        x_ref[...] = al * eye
        e_ref[...] = (1.0 - al) * eye - al * k

        def going(state):
            step, _, size = state
            return (step < 64) & (size > 1e-6)

        def level(state):
            step, rho, _ = state
            c = 2.0 / (2.0 - rho * rho)
            e = e_ref[...]
            x_ref[...] = c * (x_ref[...] + exact(x_ref[...], e))
            e = (1.0 - c) * eye_ref[...] + c * exact(e, e)
            e_ref[...] = e
            return step + 1, rho * rho / (2.0 - rho * rho), jnp.sum(e * e)

        lax.while_loop(going, level, (jnp.int32(0), mu * al * 0.5, jnp.float32(1.0)))
        e_ref[...] = exact(pt, x_ref[...])

        def refine(_, carry):
            k = kh_ref[...].astype(f32) + kl_ref[...].astype(f32)
            t = e_ref[...]
            e_ref[...] = t + exact(pt_ref[...] - t - exact(t, k), x_ref[...])
            return carry

        lax.fori_loop(0, 3, refine, 0)
        return e_ref[...]

    def phase(k, solve, hess):
        now = g_ref[k]
        ahead = g_ref[jnp.maximum(k - 1, 0)]
        eye = eye_ref[...]
        hs = split(hess)
        b = split(dot3(hs, (ph_ref[...], plo_ref[...])))
        spreads = dot3(split(apa_ref[...] / ahead[1:2]), (ath_ref[...], atl_ref[...]))
        c = dot3(hs, split(spreads[N:]))
        t = solve()
        ts = split(t)
        weights = jnp.sum(eye * now[0:1], axis=1, keepdims=True)
        kh_ref[...], kl_ref[...] = split(dot3(ts, split(c)) + weights * spreads[:N])
        th_ref[...], tl_ref[...] = ts
        bh_ref[...], bl_ref[...] = b
        column = lin_ref[...] - jnp.sum(hess * drift_ref[pl.ds(k, 1), :], axis=1, keepdims=True)
        row = jnp.sum(eye * column, axis=0, keepdims=True)
        lin_ref[...] = jnp.sum(t * row - eye * now[2:3], axis=1, keepdims=True)

    def stored_hess(k):
        product = dot3((th_ref[...], tl_ref[...]), (bh_ref[...], bl_ref[...]))
        return product + eye_ref[...] * g_ref[k][0:1]

    def sweep(solve_first, solve):
        start()
        phase(PHASES - 1, solve_first, term_ref[...])

        def body(i, carry):
            k = PHASES - 1 - i
            phase(k, solve, stored_hess(k + 1))
            return carry

        lax.fori_loop(1, PHASES - section, body, 0)

    sweep(lambda: quick(4), lambda: quick(3))

    @pl.when(jnp.max(bad_ref[...]) > 0.0)
    def _():
        sweep(careful, careful)

    height = hess_ref.shape[0]
    at = pl.multiple_of(inner * height, height)
    mine = pl.ds(at, height)
    product = dot3((th_ref[mine, :], tl_ref[mine, :]), (bh_ref[...], bl_ref[...]))
    hess_ref[...] = product + eye_ref[mine, :] * g_ref[section][0:1]
    row = jnp.sum(eye_ref[...] * lin_ref[...], axis=0, keepdims=True)
    turned = pltpu.roll(jnp.broadcast_to(-row, (8, N)), lax.rem(N - at, N), 1)
    grad_ref[...] = turned[0:1, :height]


def on_device(plant, actuation, state_weight, input_weight, state_grad, input_grad, defect, terminal_hess, terminal_grad):
    height = N // lax.axis_size("inner")
    zero = jnp.zeros((3, N), f32)
    own = jnp.concatenate([state_weight, input_weight, state_grad, input_grad, defect, zero], axis=0)
    copies = jnp.broadcast_to(own[None], (PHASES, 8, N))
    gathered = lax.all_to_all(copies, "section", split_axis=0, concat_axis=0, tiled=True)
    full = lambda dtype: pltpu.VMEM((N, N), dtype)
    hess, grad = pl.pallas_call(
        kernel,
        out_shape=(jax.ShapeDtypeStruct((height, N), f32), jax.ShapeDtypeStruct((1, height), f32)),
        in_specs=[pl.BlockSpec(memory_space=pltpu.VMEM)] * 5,
        out_specs=(pl.BlockSpec(memory_space=pltpu.VMEM),) * 2,
        scratch_shapes=[
            full(bf16), full(bf16), full(f32), full(bf16), full(bf16), full(bf16),
            pltpu.VMEM((2 * N, N), f32), full(f32), pltpu.VMEM((PHASES, N), f32),
            full(bf16), full(bf16), full(bf16), full(bf16), full(bf16), full(bf16),
            full(f32), pltpu.VMEM((N, 1), f32), pltpu.VMEM((1, 1), f32), full(f32), full(f32),
        ],
    )(gathered, plant, actuation, terminal_hess, terminal_grad[None])
    return hess[None], grad


def solution(mesh):
    data = P("section", None)
    in_specs = (P(), P(), data, data, data, data, data, P(), P())
    out_specs = (P("section", "inner", None), P("section", "inner"))
    return jax.shard_map(on_device, mesh=mesh, in_specs=in_specs, out_specs=out_specs, check_vma=False)
```

```python
import jax
import jax.numpy as jnp
from jax import lax
from jax.experimental import pallas as pl
from jax.experimental.pallas import tpu as pltpu
from jax.sharding import PartitionSpec as P

f32, bf16 = jnp.float32, jnp.bfloat16
N = 256
PHASES = 16
highest = lax.Precision.HIGHEST


def split(x):
    head = x.astype(bf16)
    return head, (x - head.astype(f32)).astype(bf16)


def dot(a, b):
    return jnp.dot(a, b, preferred_element_type=f32)


def dot3(a, b):
    (ah, al), (bh, bl) = a, b
    return dot(ah, bh) + (dot(ah, bl) + dot(al, bh))


def exact(a, b):
    return jnp.dot(a, b, precision=highest, preferred_element_type=f32)


def square_sum(x):
    return jnp.sum(jnp.sum(x * x, axis=0, keepdims=True), axis=1, keepdims=True)


def kernel(
    g_ref, plant_ref, act_ref, term_ref, tgrad_ref, hess_ref, grad_ref,
    ph_ref, plo_ref, pt_ref, pth_ref, ath_ref, atl_ref, apa_ref, eye_ref, drift_ref,
    kh_ref, kl_ref, th_ref, tl_ref, bh_ref, bl_ref, s_ref, lin_ref, bad_ref, e_ref, x_ref,
):
    section = lax.axis_index("section")
    inner = lax.axis_index("inner")
    plant = plant_ref[...]
    act = act_ref[...]
    ph_ref[...], plo_ref[...] = split(plant)
    plant_t = plant.T
    pt_ref[...] = plant_t
    pth_ref[...] = plant_t.astype(bf16)
    act_t = act.T
    ath_ref[...], atl_ref[...] = split(act_t)
    apa_ref[pl.ds(0, N), :] = act
    apa_ref[pl.ds(N, N), :] = exact(plant, act)
    rows = lax.broadcasted_iota(jnp.int32, (N, N), 0)
    cols = lax.broadcasted_iota(jnp.int32, (N, N), 1)
    eye_ref[...] = jnp.where(rows == cols, 1.0, 0.0).astype(f32)
    drift_ref[...] = g_ref[:, 4, :] - exact(g_ref[:, 3, :] / g_ref[:, 1, :], act_t)

    def start():
        eye = eye_ref[...]
        scaled = apa_ref[pl.ds(0, N), :] / g_ref[PHASES - 1][1:2]
        s = dot3(split(scaled), (ath_ref[...], atl_ref[...]))
        kh_ref[...], kl_ref[...] = split(dot3(split(term_ref[...]), split(s)))
        lin_ref[...] = -jnp.sum(eye * tgrad_ref[...], axis=1, keepdims=True)
        bad_ref[...] = jnp.zeros((1, 1), f32)

    def quick(levels, beside):
        eye, pt = eye_ref[...], pt_ref[...]
        kh, kl = kh_ref[...], kl_ref[...]
        first = dot(jnp.concatenate([kh, pth_ref[...]], axis=0), kh)
        next(beside)
        k = kh.astype(f32) + kl.astype(f32)
        mu = jnp.sqrt(square_sum(k)) * 0.25
        al = 2.0 / (2.0 + mu)
        rho = mu * al * 0.5
        c = 2.0 / (2.0 - rho * rho)
        x = eye * (c * al * (2.0 - al)) - (c * al * al) * k
        t = (c * al * (2.0 - al)) * pt - (c * al * al) * first[N:]
        e = eye * (1.0 - c + c * (1.0 - al) * (1.0 - al)) - (2.0 * c * al * (1.0 - al)) * k
        e = e + (c * al * al) * first[:N]
        for level in range(1, levels):
            rho = rho * rho / (2.0 - rho * rho)
            c = 2.0 / (2.0 - rho * rho)
            eh = e.astype(bf16)
            product = dot(jnp.concatenate([eh, x.astype(bf16), t.astype(bf16)], axis=0), eh)
            if level < 3:
                next(beside)
            e = (1.0 - c) * eye + c * product[:N]
            x = c * (x + product[N : 2 * N])
            t = c * (t + product[2 * N :])
        guess = t.astype(bf16)
        t = guess.astype(f32)
        residue = pt - t - (dot(guess, kh) + dot(guess, kl))
        next(beside)
        good = (square_sum(e) < 2.5e-3) & (square_sum(residue) < 4e-4 * square_sum(t))
        bad_ref[...] += jnp.where(good, 0.0, 1.0)
        t = t + dot(residue.astype(bf16), x.astype(bf16))
        next(beside)
        return t

    def careful(beside):
        for _ in range(5):
            next(beside)
        eye, pt = eye_ref[...], pt_ref[...]
        k = kh_ref[...].astype(f32) + kl_ref[...].astype(f32)
        most = jnp.max(jnp.sum(jnp.abs(k), axis=1, keepdims=True), axis=0, keepdims=True)
        mu = jnp.minimum(jnp.sqrt(square_sum(k)), most)
        al = 2.0 / (2.0 + mu)
        x_ref[...] = al * eye
        e_ref[...] = (1.0 - al) * eye - al * k

        def level(_, rho):
            c = 2.0 / (2.0 - rho * rho)
            e = e_ref[...]
            x_ref[...] = c * (x_ref[...] + exact(x_ref[...], e))
            e_ref[...] = (1.0 - c) * eye_ref[...] + c * exact(e, e)
            return rho * rho / (2.0 - rho * rho)

        lax.fori_loop(0, 24, level, mu * al * 0.5)
        e_ref[...] = exact(pt, x_ref[...])

        def refine(_, carry):
            k = kh_ref[...].astype(f32) + kl_ref[...].astype(f32)
            t = e_ref[...]
            e_ref[...] = t + exact(pt_ref[...] - t - exact(t, k), x_ref[...])
            return carry

        lax.fori_loop(0, 3, refine, 0)
        return e_ref[...]

    def phase(k, solve, first):
        now = g_ref[k]
        ahead = g_ref[jnp.maximum(k - 1, 0)]
        eye = eye_ref[...]
        found = {}

        def beside():
            hess = term_ref[...] if first else stored_hess(k + 1)
            yield
            act_t = ath_ref[...], atl_ref[...]
            found["ps"] = split(dot3(split(apa_ref[pl.ds(N, N), :] / ahead[1:2]), act_t))
            yield
            found["s"] = dot3(split(apa_ref[pl.ds(0, N), :] / ahead[1:2]), act_t)
            hs = split(hess)
            yield
            found["c"] = split(dot3(hs, found["ps"]))
            yield
            found["b"] = split(dot3(hs, (ph_ref[...], plo_ref[...])))
            column = lin_ref[...] - jnp.sum(hess * drift_ref[pl.ds(k, 1), :], axis=1, keepdims=True)
            found["row"] = jnp.sum(eye * column, axis=0, keepdims=True)
            yield

        t = solve(beside())
        ts = split(t)
        weights = jnp.sum(eye * now[0:1], axis=1, keepdims=True)
        kh_ref[...], kl_ref[...] = split(dot3(ts, found["c"]) + weights * found["s"])
        th_ref[...], tl_ref[...] = ts
        bh_ref[...], bl_ref[...] = found["b"]
        lin_ref[...] = jnp.sum(t * found["row"] - eye * now[2:3], axis=1, keepdims=True)

    def stored_hess(k):
        product = dot3((th_ref[...], tl_ref[...]), (bh_ref[...], bl_ref[...]))
        return product + eye_ref[...] * g_ref[k][0:1]

    def sweep(solve_first, solve):
        start()
        phase(PHASES - 1, solve_first, True)

        def body(i, carry):
            k = PHASES - 1 - i
            phase(k, solve, False)
            return carry

        lax.fori_loop(1, PHASES - section, body, 0)

    sweep(lambda side: quick(4, side), lambda side: quick(3, side))

    @pl.when(jnp.max(bad_ref[...]) > 0.0)
    def _():
        sweep(careful, careful)

    height = hess_ref.shape[0]
    at = pl.multiple_of(inner * height, height)
    mine = pl.ds(at, height)
    product = dot3((th_ref[mine, :], tl_ref[mine, :]), (bh_ref[...], bl_ref[...]))
    hess_ref[...] = product + eye_ref[mine, :] * g_ref[section][0:1]
    row = jnp.sum(eye_ref[...] * lin_ref[...], axis=0, keepdims=True)
    turned = pltpu.roll(jnp.broadcast_to(-row, (8, N)), lax.rem(N - at, N), 1)
    grad_ref[...] = turned[0:1, :height]


def recursion(*arrays_and_height):
    *arrays, height = arrays_and_height
    full = lambda dtype: pltpu.VMEM((N, N), dtype)
    return pl.pallas_call(
        kernel,
        out_shape=(jax.ShapeDtypeStruct((height, N), f32), jax.ShapeDtypeStruct((1, height), f32)),
        in_specs=[pl.BlockSpec(memory_space=pltpu.VMEM)] * 5,
        out_specs=(pl.BlockSpec(memory_space=pltpu.VMEM),) * 2,
        scratch_shapes=[
            full(bf16), full(bf16), full(f32), full(bf16), full(bf16), full(bf16),
            pltpu.VMEM((2 * N, N), f32), full(f32), pltpu.VMEM((PHASES, N), f32),
            full(bf16), full(bf16), full(bf16), full(bf16), full(bf16), full(bf16),
            full(f32), pltpu.VMEM((N, 1), f32), pltpu.VMEM((1, 1), f32), full(f32), full(f32),
        ],
    )(*arrays)


def on_device(plant, actuation, state_weight, input_weight, state_grad, input_grad, defect, terminal_hess, terminal_grad):
    height = N // lax.axis_size("inner")
    zero = jnp.zeros((3, N), f32)
    own = jnp.concatenate([state_weight, input_weight, state_grad, input_grad, defect, zero], axis=0)
    copies = jnp.broadcast_to(own[None], (PHASES, 8, N))
    gathered = lax.all_to_all(copies, "section", split_axis=0, concat_axis=0, tiled=True)
    hess, grad = recursion(gathered, plant, actuation, terminal_hess, terminal_grad[None], height)
    return hess[None], grad


def solution(mesh):
    data = P("section", None)
    in_specs = (P(), P(), data, data, data, data, data, P(), P())
    out_specs = (P("section", "inner", None), P("section", "inner"))
    return jax.shard_map(on_device, mesh=mesh, in_specs=in_specs, out_specs=out_specs, check_vma=False)
```

```python
import jax
import jax.numpy as jnp
from jax import lax
from jax.experimental import pallas as pl
from jax.experimental.pallas import tpu as pltpu
from jax.sharding import PartitionSpec as P

f32, bf16 = jnp.float32, jnp.bfloat16
N = 256
PHASES = 16
RUN = 5
highest = lax.Precision.HIGHEST


def split(x):
    head = x.astype(bf16)
    return head, (x - head.astype(f32)).astype(bf16)


def dot(a, b):
    return jnp.dot(a, b, preferred_element_type=f32)


def dot3(a, b):
    (ah, al), (bh, bl) = a, b
    return dot(jnp.concatenate([ah, ah, al], axis=1), jnp.concatenate([bh, bl, bh], axis=0))


def exact(a, b):
    return jnp.dot(a, b, precision=highest, preferred_element_type=f32)


def square_sum(x):
    return jnp.sum(jnp.sum(x * x, axis=0, keepdims=True), axis=1, keepdims=True)


def prepare(plant_ref, act_ref, ph_ref, plo_ref, pt_ref, pth_ref, ath_ref, atl_ref):
    plant = plant_ref[...]
    ph_ref[...], plo_ref[...] = split(plant)
    plant_t = plant.T
    pt_ref[...] = plant_t
    pth_ref[...] = plant_t.astype(bf16)
    ath_ref[...], atl_ref[...] = split(act_ref[...].T)


def kernel(
    g_ref, act_ref, term_ref, tgrad_ref, ph_ref, plo_ref, pt_ref, pth_ref, ath_ref, atl_ref, hess_ref, grad_ref,
    eye_ref, drift_ref,
    k_ref, kh_ref, kl_ref, hh_ref, hl_ref, sh_ref, sl_ref, s_ref, hess_all_ref, lin_all_ref, bad_ref, e_ref, x_ref,
):
    section = lax.axis_index("section")
    inner = lax.axis_index("inner")
    rows = lax.broadcasted_iota(jnp.int32, (N, N), 0)
    cols = lax.broadcasted_iota(jnp.int32, (N, N), 1)
    eye_ref[...] = jnp.where(rows == cols, 1.0, 0.0).astype(f32)
    drift_ref[...] = g_ref[:, 4, :] - exact(g_ref[:, 3, :] / g_ref[:, 1, :], ath_ref[...].astype(f32) + atl_ref[...].astype(f32))

    def start():
        hess = term_ref[...]
        hess_all_ref[PHASES] = hess
        hs = split(hess)
        hh_ref[...], hl_ref[...] = hs
        system = dot3(hs, split(spread(PHASES - 1)))
        k_ref[...] = system
        kh_ref[...], kl_ref[...] = split(system)
        s = spread(PHASES - 2)
        s_ref[...] = s
        sh_ref[...], sl_ref[...] = split(s)
        lin_all_ref[PHASES] = -jnp.sum(eye_ref[...] * tgrad_ref[...], axis=1, keepdims=True)
        bad_ref[...] = jnp.zeros((1, 1), f32)

    def quick(levels, beside):
        eye, pt = eye_ref[...], pt_ref[...]
        kh, kl = kh_ref[...], kl_ref[...]
        first = dot(jnp.concatenate([kh, pth_ref[...]], axis=0), kh)
        next(beside)
        k = k_ref[...]
        mu = jnp.sqrt(square_sum(k)) * 0.25
        al = 2.0 / (2.0 + mu)
        rho = mu * al * 0.5
        c = 2.0 / (2.0 - rho * rho)
        x = eye * (c * al * (2.0 - al)) - (c * al * al) * k
        t = (c * al * (2.0 - al)) * pt - (c * al * al) * first[N:]
        e = eye * (1.0 - c + c * (1.0 - al) * (1.0 - al)) - (2.0 * c * al * (1.0 - al)) * k
        e = e + (c * al * al) * first[:N]
        for _ in range(1, levels):
            rho = rho * rho / (2.0 - rho * rho)
            c = 2.0 / (2.0 - rho * rho)
            eh = e.astype(bf16)
            product = dot(jnp.concatenate([eh, x.astype(bf16), t.astype(bf16)], axis=0), eh)
            e = (1.0 - c) * eye + c * product[:N]
            x = c * (x + product[N : 2 * N])
            t = c * (t + product[2 * N :])
        next(beside)
        guess = t.astype(bf16)
        t = guess.astype(f32)
        residue = pt - t - dot(jnp.concatenate([guess, guess], axis=1), jnp.concatenate([kh, kl], axis=0))
        rho = rho * rho / (2.0 - rho * rho)
        c = 2.0 / (2.0 - rho * rho)
        eh = e.astype(bf16)
        product = dot(jnp.concatenate([x.astype(bf16), eh], axis=0), eh)
        x = c * (x + product[:N])
        e = (1.0 - c) * eye + c * product[N:]
        next(beside)
        t_new = t + dot(residue.astype(bf16), x.astype(bf16))
        left = square_sum(e)
        good = (left < 1e-2) & (left * square_sum(residue) < 1e-6 * square_sum(t))
        bad_ref[...] += jnp.where(good, 0.0, 1.0)
        next(beside)
        return t_new

    def careful(beside):
        for _ in range(4):
            next(beside)
        eye, pt = eye_ref[...], pt_ref[...]
        k = k_ref[...]
        most = jnp.max(jnp.sum(jnp.abs(k), axis=1, keepdims=True), axis=0, keepdims=True)
        mu = jnp.minimum(jnp.sqrt(square_sum(k)), most)
        al = 2.0 / (2.0 + mu)
        x_ref[...] = al * eye
        e_ref[...] = (1.0 - al) * eye - al * k

        def level(_, rho):
            c = 2.0 / (2.0 - rho * rho)
            e = e_ref[...]
            x_ref[...] = c * (x_ref[...] + exact(x_ref[...], e))
            e_ref[...] = (1.0 - c) * eye_ref[...] + c * exact(e, e)
            return rho * rho / (2.0 - rho * rho)

        lax.fori_loop(0, 24, level, mu * al * 0.5)
        e_ref[...] = exact(pt, x_ref[...])

        def refine(_, carry):
            k = k_ref[...]
            t = e_ref[...]
            e_ref[...] = t + exact(pt_ref[...] - t - exact(t, k), x_ref[...])
            return carry

        lax.fori_loop(0, 3, refine, 0)
        return e_ref[...]

    def spread(k):
        scaled = act_ref[...] / g_ref[jnp.maximum(k, 0)][1:2]
        return dot3(split(scaled), (ath_ref[...], atl_ref[...]))

    def phase(k, solve):
        now = g_ref[k]
        eye = eye_ref[...]
        found = {}

        def beside():
            found["b"] = split(dot3((hh_ref[...], hl_ref[...]), (ph_ref[...], plo_ref[...])))
            yield
            found["c"] = split(dot3(found["b"], (sh_ref[...], sl_ref[...])))
            yield
            product = hess_all_ref[k + 1] * drift_ref[pl.ds(k, 1), :]
            column = lin_all_ref[k + 1] - jnp.sum(product, axis=1, keepdims=True)
            found["row"] = jnp.sum(eye * column, axis=0, keepdims=True)
            found["weights"] = jnp.sum(eye * now[0:1], axis=1, keepdims=True)
            yield
            found["s"] = spread(k - 2)
            yield

        t = solve(beside())
        ts = split(t)
        system = dot3(ts, found["c"]) + found["weights"] * s_ref[...]
        k_ref[...] = system
        kh_ref[...], kl_ref[...] = split(system)
        hess = dot3(ts, found["b"]) + eye * now[0:1]
        hess_all_ref[k] = hess
        hh_ref[...], hl_ref[...] = split(hess)
        s_ref[...] = found["s"]
        sh_ref[...], sl_ref[...] = split(found["s"])
        lin_all_ref[k] = jnp.sum(t * found["row"] - eye * now[2:3], axis=1, keepdims=True)

    def sweep(solve_first, solve, run):
        start()
        phase(PHASES - 1, solve_first)

        def body(i, carry):
            for j in range(run):
                phase(PHASES - 2 - run * i - j, solve)
            return carry

        lax.fori_loop(0, (PHASES - 1) // run, body, 0)

    sweep(lambda side: quick(3, side), lambda side: quick(2, side), RUN)

    @pl.when(jnp.max(bad_ref[...]) > 0.0)
    def _():
        sweep(careful, careful, 1)

    height = hess_ref.shape[0]
    at = pl.multiple_of(inner * height, height)
    hess_ref[...] = hess_all_ref[section, pl.ds(at, height), :]
    row = jnp.sum(eye_ref[...] * lin_all_ref[section], axis=0, keepdims=True)
    turned = pltpu.roll(jnp.broadcast_to(-row, (8, N)), lax.rem(N - at, N), 1)
    grad_ref[...] = turned[0:1, :height]


def recursion(*arrays_and_height):
    *arrays, height = arrays_and_height
    full = lambda dtype: pltpu.VMEM((N, N), dtype)
    gathered, plant, actuation, terminal_hess, terminal_grad = arrays
    whole = pl.BlockSpec(memory_space=pltpu.VMEM)
    tables = pl.pallas_call(
        prepare,
        out_shape=tuple(jax.ShapeDtypeStruct((N, N), dtype) for dtype in (bf16, bf16, f32, bf16, bf16, bf16)),
        in_specs=[whole] * 2,
        out_specs=(whole,) * 6,
        cost_estimate=pl.CostEstimate(flops=1 << 20, bytes_accessed=1 << 21, transcendentals=0),
    )(plant, actuation)
    return pl.pallas_call(
        kernel,
        out_shape=(jax.ShapeDtypeStruct((height, N), f32), jax.ShapeDtypeStruct((1, height), f32)),
        in_specs=[whole] * 10,
        out_specs=(whole,) * 2,
        scratch_shapes=[
            full(f32), pltpu.VMEM((PHASES, N), f32),
            full(f32), full(bf16), full(bf16), full(bf16), full(bf16), full(bf16), full(bf16),
            full(f32), pltpu.VMEM((PHASES + 1, N, N), f32), pltpu.VMEM((PHASES + 1, N, 1), f32), pltpu.VMEM((1, 1), f32), full(f32), full(f32),
        ],
    )(gathered, actuation, terminal_hess, terminal_grad, *tables)


def on_device(plant, actuation, state_weight, input_weight, state_grad, input_grad, defect, terminal_hess, terminal_grad):
    height = N // lax.axis_size("inner")
    zero = jnp.zeros((3, N), f32)
    own = jnp.concatenate([state_weight, input_weight, state_grad, input_grad, defect, zero], axis=0)
    copies = jnp.broadcast_to(own[None], (PHASES, 8, N))
    gathered = lax.all_to_all(copies, "section", split_axis=0, concat_axis=0, tiled=True)
    hess, grad = recursion(gathered, plant, actuation, terminal_hess, terminal_grad[None], height)
    return hess[None], grad


def solution(mesh):
    data = P("section", None)
    in_specs = (P(), P(), data, data, data, data, data, P(), P())
    out_specs = (P("section", "inner", None), P("section", "inner"))
    return jax.shard_map(on_device, mesh=mesh, in_specs=in_specs, out_specs=out_specs, check_vma=False)
```

```python
import jax
import jax.numpy as jnp
from jax import lax
from jax.experimental import pallas as pl
from jax.experimental.pallas import tpu as pltpu
from jax.sharding import PartitionSpec as P

f32, bf16 = jnp.float32, jnp.bfloat16
N = 256
PHASES = 16
RUN = 5
highest = lax.Precision.HIGHEST


def split(x):
    head = x.astype(bf16)
    return head, (x - head.astype(f32)).astype(bf16)


def dot(a, b):
    return jnp.dot(a, b, preferred_element_type=f32)


def dot3(a, b):
    (ah, al), (bh, bl) = a, b
    return dot(jnp.concatenate([ah, ah, al], axis=1), jnp.concatenate([bh, bl, bh], axis=0))


def exact(a, b):
    return jnp.dot(a, b, precision=highest, preferred_element_type=f32)


def square_sum(x):
    return jnp.sum(jnp.sum(x * x, axis=0, keepdims=True), axis=1, keepdims=True)


def kernel(
    g_ref, plant_ref, act_ref, term_ref, tgrad_ref, hess_ref, grad_ref,
    ph_ref, plo_ref, pt_ref, pth_ref, ath_ref, atl_ref, eye_ref, drift_ref,
    k_ref, kh_ref, kl_ref, hh_ref, hl_ref, sh_ref, sl_ref, s_ref, hess_all_ref, lin_all_ref, bad_ref, e_ref, x_ref,
):
    section = lax.axis_index("section")
    inner = lax.axis_index("inner")
    plant = plant_ref[...]
    act = act_ref[...]
    ph_ref[...], plo_ref[...] = split(plant)
    plant_t = plant.T
    pt_ref[...] = plant_t
    pth_ref[...] = plant_t.astype(bf16)
    act_t = act.T
    ath_ref[...], atl_ref[...] = split(act_t)
    rows = lax.broadcasted_iota(jnp.int32, (N, N), 0)
    cols = lax.broadcasted_iota(jnp.int32, (N, N), 1)
    eye_ref[...] = jnp.where(rows == cols, 1.0, 0.0).astype(f32)
    drift_ref[...] = g_ref[:, 4, :] - exact(g_ref[:, 3, :] / g_ref[:, 1, :], act_t)

    def start():
        hess = term_ref[...]
        hess_all_ref[PHASES] = hess
        hs = split(hess)
        hh_ref[...], hl_ref[...] = hs
        system = dot3(hs, split(spread(PHASES - 1)))
        k_ref[...] = system
        kh_ref[...], kl_ref[...] = split(system)
        s = spread(PHASES - 2)
        s_ref[...] = s
        sh_ref[...], sl_ref[...] = split(s)
        lin_all_ref[PHASES] = -jnp.sum(eye_ref[...] * tgrad_ref[...], axis=1, keepdims=True)
        bad_ref[...] = jnp.zeros((1, 1), f32)

    def quick(levels, beside):
        eye, pt = eye_ref[...], pt_ref[...]
        kh, kl = kh_ref[...], kl_ref[...]
        first = dot(jnp.concatenate([kh, pth_ref[...]], axis=0), kh)
        next(beside)
        k = k_ref[...]
        mu = jnp.sqrt(square_sum(k)) * 0.25
        al = 2.0 / (2.0 + mu)
        rho = mu * al * 0.5
        c = 2.0 / (2.0 - rho * rho)
        x = eye * (c * al * (2.0 - al)) - (c * al * al) * k
        t = (c * al * (2.0 - al)) * pt - (c * al * al) * first[N:]
        e = eye * (1.0 - c + c * (1.0 - al) * (1.0 - al)) - (2.0 * c * al * (1.0 - al)) * k
        e = e + (c * al * al) * first[:N]
        for _ in range(1, levels):
            rho = rho * rho / (2.0 - rho * rho)
            c = 2.0 / (2.0 - rho * rho)
            eh = e.astype(bf16)
            product = dot(jnp.concatenate([eh, x.astype(bf16), t.astype(bf16)], axis=0), eh)
            e = (1.0 - c) * eye + c * product[:N]
            x = c * (x + product[N : 2 * N])
            t = c * (t + product[2 * N :])
        next(beside)
        guess = t.astype(bf16)
        t = guess.astype(f32)
        residue = pt - t - dot(jnp.concatenate([guess, guess], axis=1), jnp.concatenate([kh, kl], axis=0))
        rho = rho * rho / (2.0 - rho * rho)
        c = 2.0 / (2.0 - rho * rho)
        eh = e.astype(bf16)
        product = dot(jnp.concatenate([x.astype(bf16), eh], axis=0), eh)
        x = c * (x + product[:N])
        e = (1.0 - c) * eye + c * product[N:]
        next(beside)
        t_new = t + dot(residue.astype(bf16), x.astype(bf16))
        left = square_sum(e)
        good = (left < 1e-2) & (left * square_sum(residue) < 1e-6 * square_sum(t))
        bad_ref[...] += jnp.where(good, 0.0, 1.0)
        next(beside)
        return t_new

    def careful(beside):
        for _ in range(4):
            next(beside)
        eye, pt = eye_ref[...], pt_ref[...]
        k = k_ref[...]
        most = jnp.max(jnp.sum(jnp.abs(k), axis=1, keepdims=True), axis=0, keepdims=True)
        mu = jnp.minimum(jnp.sqrt(square_sum(k)), most)
        al = 2.0 / (2.0 + mu)
        x_ref[...] = al * eye
        e_ref[...] = (1.0 - al) * eye - al * k

        def level(_, rho):
            c = 2.0 / (2.0 - rho * rho)
            e = e_ref[...]
            x_ref[...] = c * (x_ref[...] + exact(x_ref[...], e))
            e_ref[...] = (1.0 - c) * eye_ref[...] + c * exact(e, e)
            return rho * rho / (2.0 - rho * rho)

        lax.fori_loop(0, 24, level, mu * al * 0.5)
        e_ref[...] = exact(pt, x_ref[...])

        def refine(_, carry):
            k = k_ref[...]
            t = e_ref[...]
            e_ref[...] = t + exact(pt_ref[...] - t - exact(t, k), x_ref[...])
            return carry

        lax.fori_loop(0, 3, refine, 0)
        return e_ref[...]

    def spread(k):
        scaled = act_ref[...] / g_ref[jnp.maximum(k, 0)][1:2]
        return dot3(split(scaled), (ath_ref[...], atl_ref[...]))

    def phase(k, solve):
        now = g_ref[k]
        eye = eye_ref[...]
        found = {}

        def beside():
            found["b"] = split(dot3((hh_ref[...], hl_ref[...]), (ph_ref[...], plo_ref[...])))
            yield
            found["c"] = split(dot3(found["b"], (sh_ref[...], sl_ref[...])))
            yield
            product = hess_all_ref[k + 1] * drift_ref[pl.ds(k, 1), :]
            column = lin_all_ref[k + 1] - jnp.sum(product, axis=1, keepdims=True)
            found["row"] = jnp.sum(eye * column, axis=0, keepdims=True)
            found["weights"] = jnp.sum(eye * now[0:1], axis=1, keepdims=True)
            yield
            found["s"] = spread(k - 2)
            yield

        t = solve(beside())
        ts = split(t)
        system = dot3(ts, found["c"]) + found["weights"] * s_ref[...]
        k_ref[...] = system
        kh_ref[...], kl_ref[...] = split(system)
        hess = dot3(ts, found["b"]) + eye * now[0:1]
        hess_all_ref[k] = hess
        hh_ref[...], hl_ref[...] = split(hess)
        s_ref[...] = found["s"]
        sh_ref[...], sl_ref[...] = split(found["s"])
        lin_all_ref[k] = jnp.sum(t * found["row"] - eye * now[2:3], axis=1, keepdims=True)

    def sweep(solve_first, solve, run):
        start()
        phase(PHASES - 1, solve_first)

        def body(i, carry):
            for j in range(run):
                phase(PHASES - 2 - run * i - j, solve)
            return carry

        lax.fori_loop(0, (PHASES - 1) // run, body, 0)

    sweep(lambda side: quick(3, side), lambda side: quick(2, side), RUN)

    @pl.when(jnp.max(bad_ref[...]) > 0.0)
    def _():
        sweep(careful, careful, 1)

    height = hess_ref.shape[0]
    at = pl.multiple_of(inner * height, height)
    hess_ref[...] = hess_all_ref[section, pl.ds(at, height), :]
    row = jnp.sum(eye_ref[...] * lin_all_ref[section], axis=0, keepdims=True)
    turned = pltpu.roll(jnp.broadcast_to(-row, (8, N)), lax.rem(N - at, N), 1)
    grad_ref[...] = turned[0:1, :height]


def recursion(*arrays_and_height):
    *arrays, height = arrays_and_height
    full = lambda dtype: pltpu.VMEM((N, N), dtype)
    return pl.pallas_call(
        kernel,
        out_shape=(jax.ShapeDtypeStruct((height, N), f32), jax.ShapeDtypeStruct((1, height), f32)),
        in_specs=[pl.BlockSpec(memory_space=pltpu.VMEM)] * 5,
        out_specs=(pl.BlockSpec(memory_space=pltpu.VMEM),) * 2,
        scratch_shapes=[
            full(bf16), full(bf16), full(f32), full(bf16), full(bf16), full(bf16),
            full(f32), pltpu.VMEM((PHASES, N), f32),
            full(f32), full(bf16), full(bf16), full(bf16), full(bf16), full(bf16), full(bf16),
            full(f32), pltpu.VMEM((PHASES + 1, N, N), f32), pltpu.VMEM((PHASES + 1, N, 1), f32), pltpu.VMEM((1, 1), f32), full(f32), full(f32),
        ],
    )(*arrays)


def on_device(plant, actuation, state_weight, input_weight, state_grad, input_grad, defect, terminal_hess, terminal_grad):
    height = N // lax.axis_size("inner")
    zero = jnp.zeros((3, N), f32)
    own = jnp.concatenate([state_weight, input_weight, state_grad, input_grad, defect, zero], axis=0)
    copies = jnp.broadcast_to(own[None], (PHASES, 8, N))
    gathered = lax.all_to_all(copies, "section", split_axis=0, concat_axis=0, tiled=True)
    hess, grad = recursion(gathered, plant, actuation, terminal_hess, terminal_grad[None], height)
    return hess[None], grad


def solution(mesh):
    data = P("section", None)
    in_specs = (P(), P(), data, data, data, data, data, P(), P())
    out_specs = (P("section", "inner", None), P("section", "inner"))
    return jax.shard_map(on_device, mesh=mesh, in_specs=in_specs, out_specs=out_specs, check_vma=False)
```

```python
import jax
import jax.numpy as jnp
from jax import lax
from jax.experimental import pallas as pl
from jax.experimental.pallas import tpu as pltpu
from jax.sharding import PartitionSpec as P

f32, bf16 = jnp.float32, jnp.bfloat16
N = 256
PHASES = 16
RUN = 5
highest = lax.Precision.HIGHEST


def split(x):
    head = x.astype(bf16)
    return head, (x - head.astype(f32)).astype(bf16)


def dot(a, b):
    return jnp.dot(a, b, preferred_element_type=f32)


def dot3(a, b):
    (ah, al), (bh, bl) = a, b
    return dot(jnp.concatenate([ah, ah, al], axis=1), jnp.concatenate([bh, bl, bh], axis=0))


def exact(a, b):
    return jnp.dot(a, b, precision=highest, preferred_element_type=f32)


def square_sum(x):
    return jnp.sum(jnp.sum(x * x, axis=0, keepdims=True), axis=1, keepdims=True)


def kernel(
    g_ref, plant_ref, act_ref, term_ref, tgrad_ref, hess_ref, grad_ref,
    ph_ref, plo_ref, pt_ref, pth_ref, ath_ref, atl_ref, eye_ref, drift_ref,
    k_ref, kh_ref, kl_ref, hh_ref, hl_ref, sh_ref, sl_ref, s_ref, hess_all_ref, lin_all_ref, bad_ref, e_ref, x_ref,
):
    section = lax.axis_index("section")
    inner = lax.axis_index("inner")
    plant = plant_ref[...]
    act = act_ref[...]
    ph_ref[...], plo_ref[...] = split(plant)
    plant_t = plant.T
    pt_ref[...] = plant_t
    pth_ref[...] = plant_t.astype(bf16)
    act_t = act.T
    ath_ref[...], atl_ref[...] = split(act_t)
    rows = lax.broadcasted_iota(jnp.int32, (N, N), 0)
    cols = lax.broadcasted_iota(jnp.int32, (N, N), 1)
    eye_ref[...] = jnp.where(rows == cols, 1.0, 0.0).astype(f32)
    drift_ref[...] = g_ref[:, 4, :] - exact(g_ref[:, 3, :] / g_ref[:, 1, :], act_t)

    def start():
        hess = term_ref[...]
        hess_all_ref[PHASES] = hess
        hs = split(hess)
        hh_ref[...], hl_ref[...] = hs
        system = dot3(hs, split(spread(PHASES - 1)))
        k_ref[...] = system
        kh_ref[...], kl_ref[...] = split(system)
        s = spread(PHASES - 2)
        s_ref[...] = s
        sh_ref[...], sl_ref[...] = split(s)
        lin_all_ref[PHASES] = -jnp.sum(eye_ref[...] * tgrad_ref[...], axis=1, keepdims=True)
        bad_ref[...] = jnp.zeros((1, 1), f32)

    def quick(levels, beside):
        eye, pt = eye_ref[...], pt_ref[...]
        kh, kl = kh_ref[...], kl_ref[...]
        first = dot(jnp.concatenate([kh, pth_ref[...]], axis=0), kh)
        next(beside)
        k = k_ref[...]
        mu = jnp.sqrt(square_sum(k)) * 0.25
        al = 2.0 / (2.0 + mu)
        rho = mu * al * 0.5
        c = 2.0 / (2.0 - rho * rho)
        x = eye * (c * al * (2.0 - al)) - (c * al * al) * k
        t = (c * al * (2.0 - al)) * pt - (c * al * al) * first[N:]
        e = eye * (1.0 - c + c * (1.0 - al) * (1.0 - al)) - (2.0 * c * al * (1.0 - al)) * k
        e = e + (c * al * al) * first[:N]
        for _ in range(1, levels):
            rho = rho * rho / (2.0 - rho * rho)
            c = 2.0 / (2.0 - rho * rho)
            eh = e.astype(bf16)
            product = dot(jnp.concatenate([t.astype(bf16), eh, x.astype(bf16)], axis=0), eh)
            t = c * (t + product[:N])
            e = (1.0 - c) * eye + c * product[N : 2 * N]
            x = c * (x + product[2 * N :])
        next(beside)
        guess = t.astype(bf16)
        t = guess.astype(f32)
        residue = pt - t - dot(jnp.concatenate([guess, guess], axis=1), jnp.concatenate([kh, kl], axis=0))
        rho = rho * rho / (2.0 - rho * rho)
        c = 2.0 / (2.0 - rho * rho)
        eh = e.astype(bf16)
        product = dot(jnp.concatenate([x.astype(bf16), eh], axis=0), eh)
        x = c * (x + product[:N])
        e = (1.0 - c) * eye + c * product[N:]
        next(beside)
        t_new = t + dot(residue.astype(bf16), x.astype(bf16))
        left = square_sum(e)
        good = (left < 1e-2) & (left * square_sum(residue) < 1e-6 * square_sum(t))
        bad_ref[...] += jnp.where(good, 0.0, 1.0)
        next(beside)
        return t_new

    def careful(beside):
        for _ in range(4):
            next(beside)
        eye, pt = eye_ref[...], pt_ref[...]
        k = k_ref[...]
        most = jnp.max(jnp.sum(jnp.abs(k), axis=1, keepdims=True), axis=0, keepdims=True)
        mu = jnp.minimum(jnp.sqrt(square_sum(k)), most)
        al = 2.0 / (2.0 + mu)
        x_ref[...] = al * eye
        e_ref[...] = (1.0 - al) * eye - al * k

        def level(_, rho):
            c = 2.0 / (2.0 - rho * rho)
            e = e_ref[...]
            x_ref[...] = c * (x_ref[...] + exact(x_ref[...], e))
            e_ref[...] = (1.0 - c) * eye_ref[...] + c * exact(e, e)
            return rho * rho / (2.0 - rho * rho)

        lax.fori_loop(0, 24, level, mu * al * 0.5)
        e_ref[...] = exact(pt, x_ref[...])

        def refine(_, carry):
            k = k_ref[...]
            t = e_ref[...]
            e_ref[...] = t + exact(pt_ref[...] - t - exact(t, k), x_ref[...])
            return carry

        lax.fori_loop(0, 3, refine, 0)
        return e_ref[...]

    def spread(k):
        scaled = act_ref[...] / g_ref[jnp.maximum(k, 0)][1:2]
        return dot3(split(scaled), (ath_ref[...], atl_ref[...]))

    def phase(k, solve):
        now = g_ref[k]
        eye = eye_ref[...]
        found = {}

        def beside():
            found["b"] = split(dot3((hh_ref[...], hl_ref[...]), (ph_ref[...], plo_ref[...])))
            yield
            found["c"] = split(dot3(found["b"], (sh_ref[...], sl_ref[...])))
            yield
            product = hess_all_ref[k + 1] * drift_ref[pl.ds(k, 1), :]
            column = lin_all_ref[k + 1] - jnp.sum(product, axis=1, keepdims=True)
            found["row"] = jnp.sum(eye * column, axis=0, keepdims=True)
            found["weights"] = jnp.sum(eye * now[0:1], axis=1, keepdims=True)
            yield
            found["s"] = spread(k - 2)
            yield

        t = solve(beside())
        ts = split(t)
        system = dot3(ts, found["c"]) + found["weights"] * s_ref[...]
        k_ref[...] = system
        kh_ref[...], kl_ref[...] = split(system)
        hess = dot3(ts, found["b"]) + eye * now[0:1]
        hess_all_ref[k] = hess
        hh_ref[...], hl_ref[...] = split(hess)
        s_ref[...] = found["s"]
        sh_ref[...], sl_ref[...] = split(found["s"])
        lin_all_ref[k] = jnp.sum(t * found["row"] - eye * now[2:3], axis=1, keepdims=True)

    def sweep(solve_first, solve, run):
        start()
        phase(PHASES - 1, solve_first)

        def body(i, carry):
            for j in range(run):
                phase(PHASES - 2 - run * i - j, solve)
            return carry

        lax.fori_loop(0, (PHASES - 1) // run, body, 0)

    sweep(lambda side: quick(3, side), lambda side: quick(2, side), RUN)

    @pl.when(jnp.max(bad_ref[...]) > 0.0)
    def _():
        sweep(careful, careful, 1)

    height = hess_ref.shape[0]
    at = pl.multiple_of(inner * height, height)
    hess_ref[...] = hess_all_ref[section, pl.ds(at, height), :]
    row = jnp.sum(eye_ref[...] * lin_all_ref[section], axis=0, keepdims=True)
    turned = pltpu.roll(jnp.broadcast_to(-row, (8, N)), lax.rem(N - at, N), 1)
    grad_ref[...] = turned[0:1, :height]


def recursion(*arrays_and_height):
    *arrays, height = arrays_and_height
    full = lambda dtype: pltpu.VMEM((N, N), dtype)
    return pl.pallas_call(
        kernel,
        out_shape=(jax.ShapeDtypeStruct((height, N), f32), jax.ShapeDtypeStruct((1, height), f32)),
        in_specs=[pl.BlockSpec(memory_space=pltpu.VMEM)] * 5,
        out_specs=(pl.BlockSpec(memory_space=pltpu.VMEM),) * 2,
        scratch_shapes=[
            full(bf16), full(bf16), full(f32), full(bf16), full(bf16), full(bf16),
            full(f32), pltpu.VMEM((PHASES, N), f32),
            full(f32), full(bf16), full(bf16), full(bf16), full(bf16), full(bf16), full(bf16),
            full(f32), pltpu.VMEM((PHASES + 1, N, N), f32), pltpu.VMEM((PHASES + 1, N, 1), f32), pltpu.VMEM((1, 1), f32), full(f32), full(f32),
        ],
    )(*arrays)


def on_device(plant, actuation, state_weight, input_weight, state_grad, input_grad, defect, terminal_hess, terminal_grad):
    height = N // lax.axis_size("inner")
    zero = jnp.zeros((3, N), f32)
    own = jnp.concatenate([state_weight, input_weight, state_grad, input_grad, defect, zero], axis=0)
    copies = jnp.broadcast_to(own[None], (PHASES, 8, N))
    gathered = lax.all_to_all(copies, "section", split_axis=0, concat_axis=0, tiled=True)
    hess, grad = recursion(gathered, plant, actuation, terminal_hess, terminal_grad[None], height)
    return hess[None], grad


def solution(mesh):
    data = P("section", None)
    in_specs = (P(), P(), data, data, data, data, data, P(), P())
    out_specs = (P("section", "inner", None), P("section", "inner"))
    return jax.shard_map(on_device, mesh=mesh, in_specs=in_specs, out_specs=out_specs, check_vma=False)
```
